32 devices in a mesh: rep: 2 (over y), seq: 4 (over z), head: 4 (over x, core).
Axes of the slice: x: 2, y: 2, z: 4, core: 2. Of those that a mesh axis runs over, the one named last changes fastest.
Arguments:
- queries: bfloat16 [2, 8, 64, 128], P(None, 'rep', 'head'), parts along dimension 1, may hold values from -22 to 22
- cache_keys: bfloat16 [8, 8, 4096, 128], P('rep', 'head', 'seq'), parts along dimension 0, may hold values from -15 to 15
- cache_values: bfloat16 [8, 8, 4096, 128], P('rep', 'head', 'seq'), parts along dimension 0, may hold values from -24 to 24
- new_keys: bfloat16 [2, 8, 8, 128], P(None, 'rep', 'head'), parts along dimension 1, may hold values from -12 to 12
- new_values: bfloat16 [2, 8, 8, 128], P(None, 'rep', 'head'), parts along dimension 1, may hold values from -24 to 24
- w_out: bfloat16 [8192, 8192], P('head', 'seq'), may hold values from -0.09375 to 0.09375
- lengths: int32 [8], P('rep'), parts along dimension 0, may hold values from 1024 to 4096, as said below
- positions: int32 [8], P('rep'), parts along dimension 0, may hold values from 1024 to 8192, as said below
Outputs:
- layer_out: bfloat16 [2, 8, 8192], P(None, 'rep', ('seq', 'head')), parts along dimension 1
- cache_mass: float32 [8, 8, 4096], P('rep', 'head', 'seq'), parts along dimension 0
- new_mass: float32 [8, 8, 2], P('rep', 'head'), parts along dimension 0
The draws below stay inside these ranges and needn't reach their ends.
There are 2 independent parts, one for each index of `rep`. The reference program is written for one: setup_inputs(seed, part) draws one part's arguments, and reference() takes and returns one part's arrays. A program takes and returns all parts, laid end to end along the dimension named above; an argument that names none is the same for every part. Nothing has to cross between parts.
Inputs may be any that keep to these rules, and one draw needn't show every extreme that they name: `lengths`: at least 1024; in every draw some request holds all 4096 slots. `positions`: each at least its request's cached length; the second new token stands one position further; in every draw some request's first new token stands at 8192.
All inputs are finite; a program needn't handle non-finite values.
Results may differ from the reference program's by a relative error of at most 0.013.
Values sent between devices are 32-bit elements; how exact they have to be, the bound alone decides.
A program may use at most 64 MiB of HBM per device.

```python
import math
import jax
import jax.numpy as jnp
from jax import lax

D = 8192
QH = 64
KVH = 8
HD = 128
REQ = 4
STEPS = 2
CONTEXT = 4096


def layout_plan(key):
    key_len, key_full, key_pos = jax.random.split(jax.random.fold_in(key, 7), 3)
    quarter = CONTEXT // 4
    lengths = jax.random.randint(key_len, (REQ,), quarter, CONTEXT + 1)
    full_request = jax.random.randint(key_full, (), 0, REQ)
    is_full = jnp.arange(REQ) == full_request
    lengths = jnp.where(is_full, CONTEXT, lengths).astype(jnp.int32)
    further = jax.random.randint(key_pos, (REQ,), 0, CONTEXT + 1)
    further = jnp.where(is_full, CONTEXT, further)
    positions = (lengths + further).astype(jnp.int32)
    return (lengths, positions)


def draw_lengths(key, part):
    return layout_plan(key)[0]


def draw_positions(key, part):
    return layout_plan(key)[1]


def draw_queries(key, part):
    base_key = jax.random.fold_in(key, 11)
    drawn = jnp.clip(2.5 * jax.random.normal(base_key, (STEPS, REQ, QH, HD), jnp.float32), -15.0, 15.0)
    return drawn.astype(jnp.bfloat16)


def draw_cache_keys(key, part):
    base_key = jax.random.fold_in(key, 21)
    drawn = jnp.clip(jax.random.normal(base_key, (REQ, KVH, CONTEXT, HD), jnp.float32), -6.0, 6.0)
    return drawn.astype(jnp.bfloat16)


def with_spikes(entries, key, source, target, shards_of, factor):
    owner, partner = [(jnp.arange(entries.shape[dim]) // (entries.shape[dim] // shards_of)).reshape([-1 if axis == dim else 1 for axis in range(entries.ndim)]) for dim in (source, target)]
    chosen = jax.random.permutation(key, shards_of)[partner]
    strong = (owner == chosen) | (owner == (partner + shards_of // 2) % shards_of)
    return jnp.where(strong, factor * entries, entries)


def level_of(key, dims, cuts, low, high):
    level, own = 1.0, jax.random.fold_in(key, 6)
    for axis_at, blocks in cuts:
        heights = jnp.exp(jax.random.uniform(jax.random.fold_in(own, axis_at), (blocks,), jnp.float32, low / len(cuts), high / len(cuts)))
        level = level * jnp.repeat(heights, dims[axis_at] // blocks).reshape([-1 if axis == axis_at else 1 for axis in range(len(dims))])
    return level


def scatter_about(own_key, dims, deviation, bound, pieces=(), kind=jnp.bfloat16):
    entries = jax.random.normal(own_key, dims, jnp.float32) * deviation
    if len(pieces) > 0:
        entries = level_of(own_key, dims, pieces, -0.22, 0.18) * entries
    return jnp.clip(entries, min=-bound, max=bound).astype(kind)


def noise_with(rng, shape, width, bound, shards, heavy, kind=jnp.bfloat16):
    entries = width * jax.random.normal(rng, shape, jnp.float32)
    if shards:
        entries = entries * level_of(rng, shape, shards, -0.22, 0.18)
    return jnp.clip(with_spikes(entries, jax.random.fold_in(rng, 3), *heavy), -bound, bound).astype(kind)


def setup_inputs(seed: int = 0, part: int = 0) -> dict:
    key_of = jax.random.split(jax.random.key(seed), 9)
    own_keys = jax.random.split(jax.random.fold_in(key_of[8], part), 9)
    queries = draw_queries(jax.random.fold_in(jax.random.fold_in(key_of[8], part), 71), part)
    cache_keys = draw_cache_keys(jax.random.fold_in(jax.random.fold_in(key_of[8], part), 71), part)
    cache_values = scatter_about(own_keys[2], (REQ, KVH, CONTEXT, HD), 4.0, 24.0, ((1, 4), (2, 4)))
    new_keys = scatter_about(own_keys[3], (STEPS, REQ, KVH, HD), 2.0, 12.0, ((2, 4),))
    new_values = scatter_about(own_keys[4], (STEPS, REQ, KVH, HD), 4.0, 24.0, ((2, 4),))
    w_out = noise_with(key_of[5], (QH * HD, D), (QH * HD) ** -0.5, 0.09375, ((0, 4), (1, 4)), (0, 1, 4, 2.0))
    lengths = draw_lengths(jax.random.fold_in(jax.random.fold_in(key_of[8], part), 71), part)
    positions = draw_positions(jax.random.fold_in(jax.random.fold_in(key_of[8], part), 71), part)
    return dict(queries=queries, cache_keys=cache_keys, cache_values=cache_values, new_keys=new_keys, new_values=new_values, w_out=w_out, lengths=lengths, positions=positions)


ROPE_BASE = 500000.0
FLOOR_SCORE = -1e+30

def rotate(values, turns):
    half_dim = values.shape[-1] // 2
    inv_freq = ROPE_BASE ** (-(jnp.arange(half_dim, dtype=jnp.float32) * 2.0 / values.shape[-1]))
    angles = turns[..., None] * inv_freq
    cosine = jnp.cos(angles)
    sine_part = jnp.sin(angles)
    front_half = values[..., :half_dim]
    back_half = values[..., half_dim:]
    return jnp.concatenate([front_half * cosine - back_half * sine_part, back_half * cosine + front_half * sine_part], axis=-1)

def reference(queries, cache_keys, cache_values, new_keys, new_values, w_out, lengths, positions):
    steps_n, requests, heads, head_dim = queries.shape
    kv_heads = cache_keys.shape[1]
    group_size = heads // kv_heads
    context = cache_keys.shape[2]
    offsets = jnp.arange(steps_n, dtype=jnp.int32)
    moments = (positions[None, :] + offsets[:, None]).astype(jnp.float32)
    q_turned = rotate(queries.astype(jnp.float32), moments[:, :, None]).astype(jnp.bfloat16)
    k_turned = rotate(new_keys.astype(jnp.float32), moments[:, :, None]).astype(jnp.bfloat16)
    inv_root = 1.0 / math.sqrt(head_dim)
    grouped = q_turned.astype(jnp.float32).reshape(steps_n, requests, kv_heads, group_size, head_dim)
    in_cache = jnp.arange(context, dtype=jnp.int32)[None, :] < lengths[:, None]
    cache_mask = in_cache[None, :, None, None, :]
    visible = offsets[None, :] <= offsets[:, None]
    recent_mask = visible[:, None, None, None, :]
    scores = jnp.einsum('srkgd,rktd->srkgt', grouped, cache_keys.astype(jnp.float32)) * inv_root
    scores = jnp.where(cache_mask, scores, FLOOR_SCORE)
    recent = jnp.einsum('srkgd,jrkd->srkgj', grouped, k_turned.astype(jnp.float32)) * inv_root
    recent = jnp.where(recent_mask, recent, FLOOR_SCORE)
    highest = jnp.maximum(lax.optimization_barrier(jnp.max(scores, axis=-1)), lax.optimization_barrier(jnp.max(recent, axis=-1)))
    weights = jnp.where(cache_mask, jnp.exp(scores - highest[..., None]), 0.0)
    recent_weights = jnp.where(recent_mask, jnp.exp(recent - highest[..., None]), 0.0)
    totals = lax.optimization_barrier(jnp.sum(weights, axis=-1)) + lax.optimization_barrier(jnp.sum(recent_weights, axis=-1))
    rounded = lax.optimization_barrier(weights.astype(jnp.bfloat16)).astype(jnp.float32)
    rounded_recent = lax.optimization_barrier(recent_weights.astype(jnp.bfloat16)).astype(jnp.float32)
    cache_part = jnp.einsum('srkgt,rktd->srkgd', rounded, cache_values.astype(jnp.float32))
    recent_part = jnp.einsum('srkgj,jrkd->srkgd', rounded_recent, new_values.astype(jnp.float32))
    attended = ((cache_part + recent_part) / totals[..., None]).astype(jnp.bfloat16)
    flattened = attended.reshape(steps_n * requests, heads * head_dim)
    layer_out = jnp.dot(flattened, w_out, preferred_element_type=jnp.float32).reshape(steps_n, requests, -1).astype(jnp.bfloat16)
    share = lengths.astype(jnp.float32) / (steps_n * group_size)
    cache_mass = lax.optimization_barrier(jnp.sum(weights / totals[..., None], axis=(0, 3))) * share[:, None, None]
    new_mass = lax.optimization_barrier(jnp.sum(recent_weights / totals[..., None], axis=(0, 3))) * share[:, None, None]
    return (layer_out, cache_mass, new_mass)
```

```python
import functools
import math

import jax
import jax.numpy as jnp
from jax import lax
from jax.experimental import pallas as pl
from jax.experimental.pallas import tpu as pltpu
from jax.sharding import PartitionSpec as P

ROPE_BASE = 500000.0
FLOOR_SCORE = -1e30
FLOOR_TOP = -1e29
MESH = pl.DeviceIdType.MESH


def kernel(
    seq_n, head_n, dims,
    lengths, positions, queries, new_keys, new_values, keys_hbm, values_hbm, w_hbm,
    layer_out, cache_mass, new_mass,
    keys, values, w, gathered, weights, turned, att, part, landed,
    key_sem, value_sem, w_sem, seq_send, seq_recv, head_send, head_recv,
):
    steps_n, requests, kv_here, group, head_dim, local_len = dims
    rows = steps_n * group
    half = head_dim // 2
    seq_me = lax.axis_index("seq")
    head_me = lax.axis_index("head")

    fetches = {}
    for k in range(kv_here):
        for r in range(requests):
            p = k * requests + r
            fetches["k", p] = pltpu.make_async_copy(keys_hbm.at[r, k], keys.at[p], key_sem.at[p])
            fetches["v", p] = pltpu.make_async_copy(values_hbm.at[r, k], values.at[p], value_sem.at[p])
            fetches["k", p].start()
            fetches["v", p].start()
    depth = group * head_dim
    for k in range(kv_here):
        span = pl.ds(k * depth, depth)
        fetches["w", k] = pltpu.make_async_copy(w_hbm.at[span], w.at[span], w_sem.at[k])
        fetches["w", k].start()

    barrier = pltpu.get_barrier_semaphore()
    for d in range(1, seq_n):
        pl.semaphore_signal(barrier, inc=1, device_id={"seq": lax.rem(seq_me + d, seq_n)}, device_id_type=MESH)
    for d in range(1, head_n):
        pl.semaphore_signal(barrier, inc=1, device_id={"head": lax.rem(head_me + d, head_n)}, device_id_type=MESH)

    tokens = steps_n * requests
    row_at = lax.broadcasted_iota(jnp.int32, (tokens, head_dim), 0)
    lane_at = lax.broadcasted_iota(jnp.int32, (tokens, head_dim), 1)
    turns = jnp.zeros((tokens, head_dim), jnp.float32)
    for s in range(steps_n):
        for r in range(requests):
            moment = (positions[r] + s).astype(jnp.float32)
            turns = jnp.where(row_at == s * requests + r, moment, turns)
    index = jnp.where(lane_at < half, lane_at, lane_at - half).astype(jnp.float32)
    angles = turns * jnp.exp(index * (-2.0 * math.log(ROPE_BASE) / head_dim))
    cosine = jnp.cos(angles)
    sine = jnp.sin(angles)
    sine = jnp.where(lane_at < half, -sine, sine)

    def turn(x, at):
        return x * cosine[at : at + 1] + pltpu.roll(x, half, 1) * sine[at : at + 1]

    recent = {}
    for r in range(requests):
        turned_q = [turn(queries[s, r].astype(jnp.float32), s * requests + r) for s in range(steps_n)]
        for k in range(kv_here):
            q = jnp.concatenate([t[k * group : (k + 1) * group] for t in turned_q], axis=0).astype(jnp.bfloat16)
            turned[k * requests + r] = q
    inv_root = 1.0 / math.sqrt(head_dim)

    pl.semaphore_wait(barrier, seq_n + head_n - 2)

    stat_row = requests * rows
    lane = lax.broadcasted_iota(jnp.int32, (rows, head_dim), 1)
    slots = lax.broadcasted_iota(jnp.int32, (rows, local_len), 1) + seq_me * local_len
    seq_copies = {}
    for k in range(kv_here):
        stats = jnp.zeros((rows, head_dim), jnp.float32)
        for r in range(requests):
            p = k * requests + r
            fetches["k", p].wait()
            scores = lax.dot_general(
                turned[p], keys[p], (((1,), (1,)), ((), ())), preferred_element_type=jnp.float32
            ) * inv_root
            scores = jnp.where(slots < lengths[r], scores, FLOOR_SCORE)
            top = jnp.maximum(jnp.max(scores, axis=1, keepdims=True), FLOOR_TOP)
            weight = jnp.exp(scores - top)
            weights[p] = weight
            stats = jnp.where(lane == 2 * r, top, stats)
            stats = jnp.where(lane == 2 * r + 1, jnp.sum(weight, axis=1, keepdims=True), stats)
            fetches["v", p].wait()
            gathered[seq_me, k, pl.ds(r * rows, rows), :] = jnp.dot(
                weight.astype(jnp.bfloat16), values[p], preferred_element_type=jnp.float32
            )
        gathered[seq_me, k, pl.ds(stat_row, rows), :] = stats
        for d in range(1, seq_n):
            copy = pltpu.make_async_remote_copy(
                src_ref=gathered.at[seq_me, k],
                dst_ref=gathered.at[seq_me, k],
                send_sem=seq_send.at[k, d - 1],
                recv_sem=seq_recv.at[k, d - 1],
                device_id={"seq": lax.rem(seq_me + d, seq_n)},
                device_id_type=MESH,
            )
            copy.start()
            seq_copies[k, d] = copy

    step_at = lax.broadcasted_iota(jnp.int32, (rows, 1), 0)
    for k in range(kv_here):
        for r in range(requests):
            p = k * requests + r
            q = turned[p].astype(jnp.float32)
            for i in range(steps_n):
                key = turn(new_keys[i, r].astype(jnp.float32), i * requests + r)
                key = key[k : k + 1].astype(jnp.bfloat16).astype(jnp.float32)
                score = jnp.sum(q * key, axis=1, keepdims=True) * inv_root
                recent[p, i] = jnp.where(step_at >= i * group, score, FLOOR_SCORE)

    width = part.shape[2]
    factors = {}
    head_copies = {}

    def send(d):
        copy = pltpu.make_async_remote_copy(
            src_ref=part.at[lax.rem(head_me + d, head_n)],
            dst_ref=landed.at[d - 1],
            send_sem=head_send.at[d - 1],
            recv_sem=head_recv.at[d - 1],
            device_id={"head": lax.rem(head_me + d, head_n)},
            device_id_type=MESH,
        )
        copy.start()
        head_copies[d] = copy

    whole = None
    for k in range(kv_here):
        for d in range(1, seq_n):
            seq_copies[k, d].wait()
        stat = [gathered[j, k, pl.ds(stat_row, rows), :] for j in range(seq_n)]
        own_stat = gathered[seq_me, k, pl.ds(stat_row, rows), :]
        for r in range(requests):
            p = k * requests + r
            tops = [x[:, 2 * r : 2 * r + 1] for x in stat]
            highest = functools.reduce(jnp.maximum, tops + [recent[p, i] for i in range(steps_n)])
            total = jnp.zeros((rows, 1), jnp.float32)
            mixed = jnp.zeros((rows, head_dim), jnp.float32)
            for j in range(seq_n):
                scale = jnp.exp(tops[j] - highest)
                total += scale * stat[j][:, 2 * r + 1 : 2 * r + 2]
                mixed += scale * gathered[j, k, pl.ds(r * rows, rows), :]
            recents = []
            for i in range(steps_n):
                weight = jnp.exp(recent[p, i] - highest)
                recents.append(weight)
                total += weight
                value = new_values[i, r].astype(jnp.float32)[k : k + 1]
                mixed += weight.astype(jnp.bfloat16).astype(jnp.float32) * value
            attended = mixed / total
            share = lengths[r].astype(jnp.float32) / (steps_n * group)
            factors[p] = jnp.exp(own_stat[:, 2 * r : 2 * r + 1] - highest) / total * share
            for i in range(steps_n):
                new_mass[r, k : k + 1, i : i + 1] = jnp.sum(recents[i] / total, axis=0, keepdims=True) * share
            for s in range(steps_n):
                for g in range(group):
                    att[k * group + g, pl.ds(s * requests + r, 1), :] = attended[s * group + g : s * group + g + 1]
        block = jnp.concatenate([att[k * group + g] for g in range(group)], axis=1).astype(jnp.bfloat16)
        fetches["w", k].wait()
        last = k == kv_here - 1
        if width % 128 == 0:
            for d in list(range(1, head_n)) + [0]:
                chunk = lax.rem(head_me + d, head_n)
                product = jnp.dot(
                    block,
                    w[pl.ds(k * depth, depth), pl.ds(pl.multiple_of(chunk * width, width), width)],
                    preferred_element_type=jnp.float32,
                )
                part[chunk] = product if k == 0 else part[chunk] + product
                if last and d:
                    send(d)
        else:
            product = jnp.dot(block, w[pl.ds(k * depth, depth), :], preferred_element_type=jnp.float32)
            whole = product if k == 0 else whole + product
            if last:
                for c in range(head_n):
                    part[c] = whole[:, c * width : (c + 1) * width]
                for d in range(1, head_n):
                    send(d)

    for k in range(kv_here):
        for r in range(requests):
            p = k * requests + r
            cache_mass[r, k : k + 1, :] = jnp.sum(weights[p] * factors[p], axis=0, keepdims=True)

    summed = part[head_me]
    for d in range(1, head_n):
        head_copies[d].wait()
        summed += landed[d - 1]
    for s in range(steps_n):
        layer_out[s] = summed[s * requests : (s + 1) * requests].astype(jnp.bfloat16)


def body(seq_n, head_n, queries, cache_keys, cache_values, new_keys, new_values, w_out, lengths, positions):
    steps_n, requests, heads_here, head_dim = queries.shape
    kv_here, local_len = cache_keys.shape[1:3]
    group = heads_here // kv_here
    rows = steps_n * group
    pairs = kv_here * requests
    tokens = steps_n * requests
    width = w_out.shape[1] // head_n
    vmem = pl.BlockSpec(memory_space=pltpu.VMEM)
    smem = pl.BlockSpec(memory_space=pltpu.SMEM)
    hbm = pl.BlockSpec(memory_space=pl.ANY)
    f32, bf16 = jnp.float32, jnp.bfloat16
    dma = pltpu.SemaphoreType.DMA
    return pl.pallas_call(
        functools.partial(kernel, seq_n, head_n, (steps_n, requests, kv_here, group, head_dim, local_len)),
        out_shape=(
            jax.ShapeDtypeStruct((steps_n, requests, width), bf16),
            jax.ShapeDtypeStruct((requests, kv_here, local_len), f32),
            jax.ShapeDtypeStruct((requests, kv_here, steps_n), f32),
        ),
        in_specs=[smem, smem, vmem, vmem, vmem, hbm, hbm, hbm],
        out_specs=(vmem, vmem, vmem),
        scratch_shapes=[
            pltpu.VMEM((pairs, local_len, head_dim), bf16),
            pltpu.VMEM((pairs, local_len, head_dim), bf16),
            pltpu.VMEM(w_out.shape, bf16),
            pltpu.VMEM((seq_n, kv_here, (requests + 1) * rows, head_dim), f32),
            pltpu.VMEM((pairs, rows, local_len), f32),
            pltpu.VMEM((pairs, rows, head_dim), bf16),
            pltpu.VMEM((heads_here, tokens, head_dim), f32),
            pltpu.VMEM((head_n, tokens, width), f32),
            pltpu.VMEM((head_n - 1, tokens, width), f32),
            dma((pairs,)),
            dma((pairs,)),
            dma((kv_here,)),
            dma((kv_here, seq_n - 1)),
            dma((kv_here, seq_n - 1)),
            dma((head_n - 1,)),
            dma((head_n - 1,)),
        ],
        compiler_params=pltpu.CompilerParams(collective_id=0, has_side_effects=True),
    )(lengths, positions, queries, new_keys, new_values, cache_keys, cache_values, w_out)


def solution(mesh):
    return jax.shard_map(
        functools.partial(body, mesh.shape["seq"], mesh.shape["head"]),
        mesh=mesh,
        in_specs=(
            P(None, "rep", "head", None),
            P("rep", "head", "seq", None),
            P("rep", "head", "seq", None),
            P(None, "rep", "head", None),
            P(None, "rep", "head", None),
            P("head", "seq"),
            P("rep"),
            P("rep"),
        ),
        out_specs=(
            P(None, "rep", ("seq", "head")),
            P("rep", "head", "seq"),
            P("rep", "head", None),
        ),
        check_vma=False,
    )
```

```python
import functools
import math

import jax
import jax.numpy as jnp
from jax import lax
from jax.experimental import pallas as pl
from jax.experimental.pallas import tpu as pltpu
from jax.sharding import PartitionSpec as P

ROPE_BASE = 500000.0
FLOOR_SCORE = -1e30
FLOOR_TOP = -1e29
BARRIER_AT = 0
VMEM_GRANT = 66_000_000
FINISH_GRANT = 66_000_000
MESH = pl.DeviceIdType.MESH


def kernel(
    seq_n, head_n, dims,
    lengths_hbm, positions_hbm, queries_hbm, new_keys_hbm, new_values_hbm, keys_hbm, values_hbm, w_hbm,
    layer_sum, cache_mass, new_mass,
    lengths, positions, queries, new_keys, new_values, keys, values, w, gathered, weights, turned, att, part, landed,
    small_sem, key_sem, value_sem, w_sem, seq_send, seq_recv, head_send, head_recv,
):
    steps_n, requests, kv_here, group, head_dim, local_len = dims
    rows = steps_n * group
    half = head_dim // 2
    seq_me = lax.axis_index("seq")
    head_me = lax.axis_index("head")

    smalls = [
        pltpu.make_async_copy(source, target, small_sem.at[n])
        for n, (source, target) in enumerate(zip(
            (positions_hbm, lengths_hbm, queries_hbm, new_keys_hbm, new_values_hbm),
            (positions, lengths, queries, new_keys, new_values),
        ))
    ]
    for copy in smalls:
        copy.start()
    barrier = pltpu.get_barrier_semaphore()
    for d in range(1, seq_n):
        pl.semaphore_signal(barrier, inc=1, device_id={"seq": lax.rem(seq_me + d, seq_n)}, device_id_type=MESH)
    for d in range(1, head_n):
        pl.semaphore_signal(barrier, inc=1, device_id={"head": lax.rem(head_me + d, head_n)}, device_id_type=MESH)
    fetches = {}
    for k in range(kv_here):
        for r in range(requests):
            p = k * requests + r
            fetches["k", p] = pltpu.make_async_copy(keys_hbm.at[r, k], keys.at[p], key_sem.at[p])
            fetches["v", p] = pltpu.make_async_copy(values_hbm.at[r, k], values.at[p], value_sem.at[p])
            fetches["k", p].start()
            fetches["v", p].start()
    depth = group * head_dim
    for k in range(kv_here):
        span = pl.ds(k * depth, depth)
        fetches["w", k] = pltpu.make_async_copy(w_hbm.at[span], w.at[span], w_sem.at[k])
        fetches["w", k].start()

    for copy in smalls:
        copy.wait()

    tokens = steps_n * requests
    row_at = lax.broadcasted_iota(jnp.int32, (tokens, head_dim), 0)
    lane_at = lax.broadcasted_iota(jnp.int32, (tokens, head_dim), 1)
    turns = jnp.zeros((tokens, head_dim), jnp.float32)
    for s in range(steps_n):
        for r in range(requests):
            moment = (positions[r] + s).astype(jnp.float32)
            turns = jnp.where(row_at == s * requests + r, moment, turns)
    index = jnp.where(lane_at < half, lane_at, lane_at - half).astype(jnp.float32)
    angles = turns * jnp.exp(index * (-2.0 * math.log(ROPE_BASE) / head_dim))
    cosine = jnp.cos(angles)
    sine = jnp.sin(angles)
    sine = jnp.where(lane_at < half, -sine, sine)

    def turn(x, at):
        return x * cosine[at : at + 1] + pltpu.roll(x, half, 1) * sine[at : at + 1]

    recent = {}
    for r in range(requests):
        turned_q = [turn(queries[s, r].astype(jnp.float32), s * requests + r) for s in range(steps_n)]
        for k in range(kv_here):
            q = jnp.concatenate([t[k * group : (k + 1) * group] for t in turned_q], axis=0).astype(jnp.bfloat16)
            turned[k * requests + r] = q
    inv_root = 1.0 / math.sqrt(head_dim)

    stat_row = requests * rows
    lane = lax.broadcasted_iota(jnp.int32, (group, head_dim), 1)
    slots = lax.broadcasted_iota(jnp.int32, (rows, local_len), 1) + seq_me * local_len
    seq_copies = {}

    def share_piece(k, r):
        p = k * requests + r
        piece = gathered.at[seq_me, k, pl.ds(r * rows, rows if r < requests - 1 else rows + group)]
        for d in range(1, seq_n):
            copy = pltpu.make_async_remote_copy(
                src_ref=piece,
                dst_ref=piece,
                send_sem=seq_send.at[p, d - 1],
                recv_sem=seq_recv.at[p, d - 1],
                device_id={"seq": lax.rem(seq_me + d, seq_n)},
                device_id_type=MESH,
            )
            copy.start()
            seq_copies[p, d] = copy

    for k in range(kv_here):
        stats = jnp.zeros((group, head_dim), jnp.float32)
        for r in range(requests):
            p = k * requests + r
            fetches["k", p].wait()
            scores = lax.dot_general(
                turned[p], keys[p], (((1,), (1,)), ((), ())), preferred_element_type=jnp.float32
            ) * inv_root
            scores = jnp.where(slots < lengths[r], scores, FLOOR_SCORE)
            top = jnp.maximum(jnp.max(scores, axis=1, keepdims=True), FLOOR_TOP)
            weight = jnp.exp(scores - top)
            weights[p] = weight
            total = jnp.sum(weight, axis=1, keepdims=True)
            for s in range(steps_n):
                column = 2 * (s * requests + r)
                own = slice(s * group, (s + 1) * group)
                stats = jnp.where(lane == column, top[own], stats)
                stats = jnp.where(lane == column + 1, total[own], stats)
            fetches["v", p].wait()
            gathered[seq_me, k, pl.ds(r * rows, rows), :] = jnp.dot(
                weight.astype(jnp.bfloat16), values[p], preferred_element_type=jnp.float32
            )
            if r == requests - 1:
                gathered[seq_me, k, pl.ds(stat_row, group), :] = stats
            if p == BARRIER_AT:
                pl.semaphore_wait(barrier, seq_n + head_n - 2)
                for earlier in range(p + 1):
                    share_piece(*divmod(earlier, requests))
            if p > BARRIER_AT:
                share_piece(k, r)

    step_at = lax.broadcasted_iota(jnp.int32, (rows, 1), 0)
    for k in range(kv_here):
        for r in range(requests):
            p = k * requests + r
            q = turned[p].astype(jnp.float32)
            for i in range(steps_n):
                key = turn(new_keys[i, r].astype(jnp.float32), i * requests + r)
                key = key[k : k + 1].astype(jnp.bfloat16).astype(jnp.float32)
                score = jnp.sum(q * key, axis=1, keepdims=True) * inv_root
                recent[p, i] = jnp.where(step_at >= i * group, score, FLOOR_SCORE)

    width = part.shape[2]
    factors = {}
    head_copies = {}

    def send(d):
        copy = pltpu.make_async_remote_copy(
            src_ref=part.at[lax.rem(head_me + d, head_n)],
            dst_ref=landed.at[d - 1],
            send_sem=head_send.at[d - 1],
            recv_sem=head_recv.at[d - 1],
            device_id={"head": lax.rem(head_me + d, head_n)},
            device_id_type=MESH,
        )
        copy.start()
        head_copies[d] = copy

    def column_of(stat, r, which):
        at = [2 * (s * requests + r) + which for s in range(steps_n)]
        return jnp.concatenate([stat[:, c : c + 1] for c in at], axis=0)

    whole = None
    for k in range(kv_here):
        for r in range(requests):
            for d in range(1, seq_n):
                seq_copies[k * requests + r, d].wait()
        stat = [gathered[j, k, pl.ds(stat_row, group), :] for j in range(seq_n)]
        own_stat = gathered[seq_me, k, pl.ds(stat_row, group), :]
        for r in range(requests):
            p = k * requests + r
            tops = [column_of(x, r, 0) for x in stat]
            highest = functools.reduce(jnp.maximum, tops + [recent[p, i] for i in range(steps_n)])
            total = jnp.zeros((rows, 1), jnp.float32)
            mixed = jnp.zeros((rows, head_dim), jnp.float32)
            for j in range(seq_n):
                scale = jnp.exp(tops[j] - highest)
                total += scale * column_of(stat[j], r, 1)
                mixed += scale * gathered[j, k, pl.ds(r * rows, rows), :]
            recents = []
            for i in range(steps_n):
                weight = jnp.exp(recent[p, i] - highest)
                recents.append(weight)
                total += weight
                value = new_values[i, r].astype(jnp.float32)[k : k + 1]
                mixed += weight.astype(jnp.bfloat16).astype(jnp.float32) * value
            attended = mixed / total
            share = lengths[r].astype(jnp.float32) / (steps_n * group)
            factors[p] = jnp.exp(column_of(own_stat, r, 0) - highest) / total * share
            for i in range(steps_n):
                new_mass[k, i : i + 1, r : r + 1] = jnp.sum(recents[i] / total, axis=0, keepdims=True) * share
            for s in range(steps_n):
                for g in range(group):
                    att[k * group + g, pl.ds(s * requests + r, 1), :] = attended[s * group + g : s * group + g + 1]
        block = jnp.concatenate([att[k * group + g] for g in range(group)], axis=1).astype(jnp.bfloat16)
        fetches["w", k].wait()
        last = k == kv_here - 1
        if width % 128 == 0:
            for d in list(range(1, head_n)) + [0]:
                chunk = lax.rem(head_me + d, head_n)
                product = jnp.dot(
                    block,
                    w[pl.ds(k * depth, depth), pl.ds(pl.multiple_of(chunk * width, width), width)],
                    preferred_element_type=jnp.float32,
                )
                part[chunk] = product if k == 0 else part[chunk] + product
                if last and d:
                    send(d)
        else:
            product = jnp.dot(block, w[pl.ds(k * depth, depth), :], preferred_element_type=jnp.float32)
            whole = product if k == 0 else whole + product
            if last:
                for c in range(head_n):
                    part[c] = whole[:, c * width : (c + 1) * width]
                for d in range(1, head_n):
                    send(d)

    for k in range(kv_here):
        for r in range(requests):
            p = k * requests + r
            cache_mass[r, k : k + 1, :] = jnp.sum(weights[p] * factors[p], axis=0, keepdims=True)

    summed = part[head_me]
    for d in range(1, head_n):
        head_copies[d].wait()
        summed += landed[d - 1]
    layer_sum[...] = summed


def finish(layer_sum, mass_in, new_in, layer_out, cache_mass, new_mass):
    steps_n, requests = layer_out.shape[:2]
    for s in range(steps_n):
        layer_out[s] = layer_sum[s * requests : (s + 1) * requests].astype(jnp.bfloat16)
    cache_mass[...] = mass_in[...]
    new_mass[...] = new_in[...]


def body(seq_n, head_n, queries, cache_keys, cache_values, new_keys, new_values, w_out, lengths, positions):
    steps_n, requests, heads_here, head_dim = queries.shape
    kv_here, local_len = cache_keys.shape[1:3]
    group = heads_here // kv_here
    rows = steps_n * group
    pairs = kv_here * requests
    tokens = steps_n * requests
    width = w_out.shape[1] // head_n
    vmem = pl.BlockSpec(memory_space=pltpu.VMEM)
    hbm = pl.BlockSpec(memory_space=pltpu.HBM)
    f32, bf16 = jnp.float32, jnp.bfloat16
    dma = pltpu.SemaphoreType.DMA
    summed, cache_mass, new_mass = pl.pallas_call(
        functools.partial(kernel, seq_n, head_n, (steps_n, requests, kv_here, group, head_dim, local_len)),
        out_shape=(
            jax.ShapeDtypeStruct((tokens, width), f32),
            jax.ShapeDtypeStruct((requests, kv_here, local_len), f32),
            jax.ShapeDtypeStruct((kv_here, steps_n, requests), f32),
        ),
        in_specs=[hbm] * 8,
        out_specs=(vmem, vmem, vmem),
        scratch_shapes=[
            pltpu.SMEM(lengths.shape, jnp.int32),
            pltpu.SMEM(positions.shape, jnp.int32),
            pltpu.VMEM(queries.shape, bf16),
            pltpu.VMEM(new_keys.shape, bf16),
            pltpu.VMEM(new_values.shape, bf16),
            pltpu.VMEM((pairs, local_len, head_dim), bf16),
            pltpu.VMEM((pairs, local_len, head_dim), bf16),
            pltpu.VMEM(w_out.shape, bf16),
            pltpu.VMEM((seq_n, kv_here, requests * rows + group, head_dim), f32),
            pltpu.VMEM((pairs, rows, local_len), f32),
            pltpu.VMEM((pairs, rows, head_dim), bf16),
            pltpu.VMEM((heads_here, tokens, head_dim), f32),
            pltpu.VMEM((head_n, tokens, width), f32),
            pltpu.VMEM((head_n - 1, tokens, width), f32),
            dma((5,)),
            dma((pairs,)),
            dma((pairs,)),
            dma((kv_here,)),
            dma((pairs, seq_n - 1)),
            dma((pairs, seq_n - 1)),
            dma((head_n - 1,)),
            dma((head_n - 1,)),
        ],
        compiler_params=pltpu.CompilerParams(
            collective_id=0, has_side_effects=True, vmem_limit_bytes=VMEM_GRANT
        ),
    )(lengths, positions, queries, new_keys, new_values, cache_keys, cache_values, w_out)
    layer_out, cache_mass, new_mass = pl.pallas_call(
        finish,
        out_shape=(
            jax.ShapeDtypeStruct((steps_n, requests, width), bf16),
            jax.ShapeDtypeStruct(cache_mass.shape, f32),
            jax.ShapeDtypeStruct(new_mass.shape, f32),
        ),
        in_specs=[vmem] * 3,
        out_specs=(vmem, vmem, vmem),
        compiler_params=pltpu.CompilerParams(vmem_limit_bytes=FINISH_GRANT),
    )(summed, cache_mass, new_mass)
    return layer_out, cache_mass, jnp.transpose(new_mass, (2, 0, 1))


def solution(mesh):
    return jax.shard_map(
        functools.partial(body, mesh.shape["seq"], mesh.shape["head"]),
        mesh=mesh,
        in_specs=(
            P(None, "rep", "head", None),
            P("rep", "head", "seq", None),
            P("rep", "head", "seq", None),
            P(None, "rep", "head", None),
            P(None, "rep", "head", None),
            P("head", "seq"),
            P("rep"),
            P("rep"),
        ),
        out_specs=(
            P(None, "rep", ("seq", "head")),
            P("rep", "head", "seq"),
            P("rep", "head", None),
        ),
        check_vma=False,
    )
```

```python
import functools
import math

import jax
import jax.numpy as jnp
from jax import lax
from jax.experimental import pallas as pl
from jax.experimental.pallas import tpu as pltpu
from jax.sharding import PartitionSpec as P

ROPE_BASE = 500000.0
FLOOR_SCORE = -1e30
FLOOR_TOP = -1e29
BARRIER_AT = 0
FETCH_AT = 0
VMEM_GRANT = 64_000_000
FINISH_GRANT = 8_000_000
MESH = pl.DeviceIdType.MESH


def far_first(n):
    return sorted(range(1, n), key=lambda d: -min(d, n - d))


def kernel(
    seq_n, head_n, dims,
    lengths_hbm, positions_hbm, queries_hbm, new_keys_hbm, new_values_hbm, keys_hbm, values_hbm, w_hbm,
    layer_sum, cache_mass, new_mass,
    lengths, positions, queries, new_keys, new_values, keys, values, w, gathered, weights, turned, att, part, landed,
    small_sem, key_sem, value_sem, w_sem, seq_send, seq_recv, head_send, head_recv,
):
    steps_n, requests, kv_here, group, head_dim, local_len = dims
    rows = steps_n * group
    half = head_dim // 2
    seq_me = lax.axis_index("seq")
    head_me = lax.axis_index("head")

    smalls = [
        pltpu.make_async_copy(source, target, small_sem.at[n])
        for n, (source, target) in enumerate(zip(
            (positions_hbm, lengths_hbm, queries_hbm, new_keys_hbm, new_values_hbm),
            (positions, lengths, queries, new_keys, new_values),
        ))
    ]
    for copy in smalls:
        copy.start()
    barrier = pltpu.get_barrier_semaphore()
    for d in range(1, seq_n):
        pl.semaphore_signal(barrier, inc=1, device_id={"seq": lax.rem(seq_me + d, seq_n)}, device_id_type=MESH)
    for d in range(1, head_n):
        pl.semaphore_signal(barrier, inc=1, device_id={"head": lax.rem(head_me + d, head_n)}, device_id_type=MESH)
    fetches = {}
    for k in range(kv_here):
        for r in range(requests):
            p = k * requests + r
            fetches["k", p] = pltpu.make_async_copy(keys_hbm.at[r, k], keys.at[p], key_sem.at[p])
            fetches["v", p] = pltpu.make_async_copy(values_hbm.at[r, k], values.at[p], value_sem.at[p])
            fetches["k", p].start()
            fetches["v", p].start()
    depth = group * head_dim
    for k in range(kv_here):
        span = pl.ds(k * depth, depth)
        fetches["w", k] = pltpu.make_async_copy(w_hbm.at[span], w.at[span], w_sem.at[k])

    for copy in smalls:
        copy.wait()

    tokens = steps_n * requests
    row_at = lax.broadcasted_iota(jnp.int32, (tokens, head_dim), 0)
    lane_at = lax.broadcasted_iota(jnp.int32, (tokens, head_dim), 1)
    turns = jnp.zeros((tokens, head_dim), jnp.float32)
    for s in range(steps_n):
        for r in range(requests):
            moment = (positions[r] + s).astype(jnp.float32)
            turns = jnp.where(row_at == s * requests + r, moment, turns)
    index = jnp.where(lane_at < half, lane_at, lane_at - half).astype(jnp.float32)
    angles = turns * jnp.exp(index * (-2.0 * math.log(ROPE_BASE) / head_dim))
    cosine = jnp.cos(angles)
    sine = jnp.sin(angles)
    sine = jnp.where(lane_at < half, -sine, sine)

    def turn(x, at):
        return x * cosine[at : at + 1] + pltpu.roll(x, half, 1) * sine[at : at + 1]

    recent = {}
    for r in range(requests):
        turned_q = [turn(queries[s, r].astype(jnp.float32), s * requests + r) for s in range(steps_n)]
        for k in range(kv_here):
            q = jnp.concatenate([t[k * group : (k + 1) * group] for t in turned_q], axis=0).astype(jnp.bfloat16)
            turned[k * requests + r] = q
    inv_root = 1.0 / math.sqrt(head_dim)

    stat_row = requests * rows
    lane = lax.broadcasted_iota(jnp.int32, (group, head_dim), 1)
    slots = lax.broadcasted_iota(jnp.int32, (rows, local_len), 1) + seq_me * local_len
    seq_copies = {}

    def share_piece(k, r):
        p = k * requests + r
        piece = gathered.at[seq_me, k, pl.ds(r * rows, rows if r < requests - 1 else rows + group)]
        for d in far_first(seq_n):
            copy = pltpu.make_async_remote_copy(
                src_ref=piece,
                dst_ref=piece,
                send_sem=seq_send.at[p, d - 1],
                recv_sem=seq_recv.at[p, d - 1],
                device_id={"seq": lax.rem(seq_me + d, seq_n)},
                device_id_type=MESH,
            )
            copy.start()
            seq_copies[p, d] = copy

    for k in range(kv_here):
        stats = jnp.zeros((group, head_dim), jnp.float32)
        for r in range(requests):
            p = k * requests + r
            fetches["k", p].wait()
            if p == FETCH_AT:
                for n in range(kv_here):
                    fetches["w", n].start()
            scores = lax.dot_general(
                turned[p], keys[p], (((1,), (1,)), ((), ())), preferred_element_type=jnp.float32
            ) * inv_root
            scores = jnp.where(slots < lengths[r], scores, FLOOR_SCORE)
            top = jnp.maximum(jnp.max(scores, axis=1, keepdims=True), FLOOR_TOP)
            weight = jnp.exp(scores - top)
            weights[p] = weight
            total = jnp.sum(weight, axis=1, keepdims=True)
            for s in range(steps_n):
                column = 2 * (s * requests + r)
                own = slice(s * group, (s + 1) * group)
                stats = jnp.where(lane == column, top[own], stats)
                stats = jnp.where(lane == column + 1, total[own], stats)
            fetches["v", p].wait()
            gathered[seq_me, k, pl.ds(r * rows, rows), :] = jnp.dot(
                weight.astype(jnp.bfloat16), values[p], preferred_element_type=jnp.float32
            )
            if r == requests - 1:
                gathered[seq_me, k, pl.ds(stat_row, group), :] = stats
            if p == BARRIER_AT:
                pl.semaphore_wait(barrier, seq_n + head_n - 2)
                for earlier in range(p + 1):
                    share_piece(*divmod(earlier, requests))
            if p > BARRIER_AT:
                share_piece(k, r)

    step_at = lax.broadcasted_iota(jnp.int32, (rows, 1), 0)
    for k in range(kv_here):
        for r in range(requests):
            p = k * requests + r
            q = turned[p].astype(jnp.float32)
            for i in range(steps_n):
                key = turn(new_keys[i, r].astype(jnp.float32), i * requests + r)
                key = key[k : k + 1].astype(jnp.bfloat16).astype(jnp.float32)
                score = jnp.sum(q * key, axis=1, keepdims=True) * inv_root
                recent[p, i] = jnp.where(step_at >= i * group, score, FLOOR_SCORE)

    width = part.shape[2]
    factors = {}
    head_copies = {}

    def send(d):
        copy = pltpu.make_async_remote_copy(
            src_ref=part.at[lax.rem(head_me + d, head_n)],
            dst_ref=landed.at[d - 1],
            send_sem=head_send.at[d - 1],
            recv_sem=head_recv.at[d - 1],
            device_id={"head": lax.rem(head_me + d, head_n)},
            device_id_type=MESH,
        )
        copy.start()
        head_copies[d] = copy

    def column_of(stat, r, which):
        at = [2 * (s * requests + r) + which for s in range(steps_n)]
        return jnp.concatenate([stat[:, c : c + 1] for c in at], axis=0)

    whole = None
    for k in range(kv_here):
        for r in range(requests):
            for d in range(1, seq_n):
                seq_copies[k * requests + r, d].wait()
        stat = [gathered[j, k, pl.ds(stat_row, group), :] for j in range(seq_n)]
        own_stat = gathered[seq_me, k, pl.ds(stat_row, group), :]
        for r in range(requests):
            p = k * requests + r
            tops = [column_of(x, r, 0) for x in stat]
            highest = functools.reduce(jnp.maximum, tops + [recent[p, i] for i in range(steps_n)])
            total = jnp.zeros((rows, 1), jnp.float32)
            mixed = jnp.zeros((rows, head_dim), jnp.float32)
            for j in range(seq_n):
                scale = jnp.exp(tops[j] - highest)
                total += scale * column_of(stat[j], r, 1)
                mixed += scale * gathered[j, k, pl.ds(r * rows, rows), :]
            recents = []
            for i in range(steps_n):
                weight = jnp.exp(recent[p, i] - highest)
                recents.append(weight)
                total += weight
                value = new_values[i, r].astype(jnp.float32)[k : k + 1]
                mixed += weight.astype(jnp.bfloat16).astype(jnp.float32) * value
            attended = mixed / total
            share = lengths[r].astype(jnp.float32) / (steps_n * group)
            factors[p] = jnp.exp(column_of(own_stat, r, 0) - highest) / total * share
            for i in range(steps_n):
                new_mass[k, i : i + 1, r : r + 1] = jnp.sum(recents[i] / total, axis=0, keepdims=True) * share
            for s in range(steps_n):
                for g in range(group):
                    att[k * group + g, pl.ds(s * requests + r, 1), :] = attended[s * group + g : s * group + g + 1]
        block = jnp.concatenate([att[k * group + g] for g in range(group)], axis=1).astype(jnp.bfloat16)
        fetches["w", k].wait()
        last = k == kv_here - 1
        if width % 128 == 0:
            for d in list(range(1, head_n)) + [0]:
                chunk = lax.rem(head_me + d, head_n)
                product = jnp.dot(
                    block,
                    w[pl.ds(k * depth, depth), pl.ds(pl.multiple_of(chunk * width, width), width)],
                    preferred_element_type=jnp.float32,
                )
                part[chunk] = product if k == 0 else part[chunk] + product
                if last and d:
                    send(d)
        else:
            product = jnp.dot(block, w[pl.ds(k * depth, depth), :], preferred_element_type=jnp.float32)
            whole = product if k == 0 else whole + product
            if last:
                for c in range(head_n):
                    part[c] = whole[:, c * width : (c + 1) * width]
                for d in range(1, head_n):
                    send(d)

    for k in range(kv_here):
        for r in range(requests):
            p = k * requests + r
            cache_mass[r, k : k + 1, :] = jnp.sum(weights[p] * factors[p], axis=0, keepdims=True)

    summed = part[head_me]
    for d in range(1, head_n):
        head_copies[d].wait()
        summed += landed[d - 1]
    layer_sum[...] = summed


def finish(layer_sum, mass_in, new_in, layer_out, cache_mass, new_mass):
    steps_n, requests = layer_out.shape[:2]
    for s in range(steps_n):
        layer_out[s] = layer_sum[s * requests : (s + 1) * requests].astype(jnp.bfloat16)
    cache_mass[...] = mass_in[...]
    new_mass[...] = new_in[...]


def body(seq_n, head_n, queries, cache_keys, cache_values, new_keys, new_values, w_out, lengths, positions):
    steps_n, requests, heads_here, head_dim = queries.shape
    kv_here, local_len = cache_keys.shape[1:3]
    group = heads_here // kv_here
    rows = steps_n * group
    pairs = kv_here * requests
    tokens = steps_n * requests
    width = w_out.shape[1] // head_n
    vmem = pl.BlockSpec(memory_space=pltpu.VMEM)
    hbm = pl.BlockSpec(memory_space=pltpu.HBM)
    f32, bf16 = jnp.float32, jnp.bfloat16
    dma = pltpu.SemaphoreType.DMA
    summed, cache_mass, new_mass = pl.pallas_call(
        functools.partial(kernel, seq_n, head_n, (steps_n, requests, kv_here, group, head_dim, local_len)),
        out_shape=(
            pltpu.VMEM((tokens, width), f32),
            pltpu.VMEM((requests, kv_here, local_len), f32),
            pltpu.VMEM((kv_here, steps_n, requests), f32),
        ),
        in_specs=[hbm] * 8,
        out_specs=(vmem, vmem, vmem),
        scratch_shapes=[
            pltpu.SMEM(lengths.shape, jnp.int32),
            pltpu.SMEM(positions.shape, jnp.int32),
            pltpu.VMEM(queries.shape, bf16),
            pltpu.VMEM(new_keys.shape, bf16),
            pltpu.VMEM(new_values.shape, bf16),
            pltpu.VMEM((pairs, local_len, head_dim), bf16),
            pltpu.VMEM((pairs, local_len, head_dim), bf16),
            pltpu.VMEM(w_out.shape, bf16),
            pltpu.VMEM((seq_n, kv_here, requests * rows + group, head_dim), f32),
            pltpu.VMEM((pairs, rows, local_len), f32),
            pltpu.VMEM((pairs, rows, head_dim), bf16),
            pltpu.VMEM((heads_here, tokens, head_dim), f32),
            pltpu.VMEM((head_n, tokens, width), f32),
            pltpu.VMEM((head_n - 1, tokens, width), f32),
            dma((5,)),
            dma((pairs,)),
            dma((pairs,)),
            dma((kv_here,)),
            dma((pairs, seq_n - 1)),
            dma((pairs, seq_n - 1)),
            dma((head_n - 1,)),
            dma((head_n - 1,)),
        ],
        compiler_params=pltpu.CompilerParams(
            collective_id=0, has_side_effects=True, vmem_limit_bytes=VMEM_GRANT
        ),
    )(lengths, positions, queries, new_keys, new_values, cache_keys, cache_values, w_out)
    layer_out, cache_mass, new_mass = pl.pallas_call(
        finish,
        out_shape=(
            jax.ShapeDtypeStruct((steps_n, requests, width), bf16),
            jax.ShapeDtypeStruct(cache_mass.shape, f32),
            jax.ShapeDtypeStruct(new_mass.shape, f32),
        ),
        in_specs=[vmem] * 3,
        out_specs=(vmem, vmem, vmem),
        compiler_params=pltpu.CompilerParams(vmem_limit_bytes=FINISH_GRANT),
    )(summed, cache_mass, new_mass)
    return layer_out, cache_mass, jnp.transpose(new_mass, (2, 0, 1))


def solution(mesh):
    return jax.shard_map(
        functools.partial(body, mesh.shape["seq"], mesh.shape["head"]),
        mesh=mesh,
        in_specs=(
            P(None, "rep", "head", None),
            P("rep", "head", "seq", None),
            P("rep", "head", "seq", None),
            P(None, "rep", "head", None),
            P(None, "rep", "head", None),
            P("head", "seq"),
            P("rep"),
            P("rep"),
        ),
        out_specs=(
            P(None, "rep", ("seq", "head")),
            P("rep", "head", "seq"),
            P("rep", "head", None),
        ),
        check_vma=False,
    )
```
